512 devices in a mesh: gz: 64 (over y, x, core), gy: 8 (over z).
Axes of the slice: x: 4, y: 8, z: 8, core: 2. Of those that a mesh axis runs over, the one named last changes fastest.
Arguments:
- scalar: float32 [128, 512, 1024], P('gz', 'gy'), as said below
- bin_index: int32 [128, 512, 1024], P('gz', 'gy'), may hold values from 0 to 255, as said below
- color_table: bfloat16 [3, 257], replicated, may hold values from 0.099609375 to 1
- opacity_table: bfloat16 [257], replicated, may hold values from 0.00049972534 to 0.019897461
- light_dir: float32 [3], replicated, may hold values from -4 to 4
- view_order: int32 [64], replicated, may hold values from 0 to 63, each once
Outputs:
- image_rgba: float32 [4, 8, 64, 1024], P(None, 'gy', 'gz')
The draws below stay inside these ranges and needn't reach their ends.
Inputs may be any that keep to these rules, and one draw needn't show every extreme that they name: bin_index is the floor of 256 scalar in every cell, except that fraction may reach 1. scalar lies between bin_index / 256 and (bin_index + 1) / 256. `view_order`: each brick position appears once.
All inputs are finite; a program needn't handle non-finite values.
Results may differ from the reference program's by a relative error of at most 0.0003.
Values sent between devices are 32-bit elements; how exact they have to be, the bound alone decides.
A program may use at most 64 MiB of HBM per device.

```python
import math
import jax
import jax.numpy as jnp
from jax import lax

W = 1024
NBINS = 256
DZ = 2
RY = 64
NZ = 128
NY = 512
N_GZ = 64
N_GY = 8


def draw_codes(key):
    return jax.random.randint(jax.random.fold_in(key, 7), (NZ, NY, W), 0, NBINS, dtype=jnp.int32)


def draw_bin_index(key, part):
    return draw_codes(key)


def draw_scalar(key, part):
    bin_codes = draw_codes(key)
    inside = jax.random.uniform(jax.random.fold_in(key, 11), (NZ, NY, W), jnp.float32)
    return (bin_codes.astype(jnp.float32) + inside) / NBINS


def bell_draw(key, dims, deviation, limit, kind=jnp.bfloat16):
    array = deviation * jax.random.normal(key, dims, jnp.float32)
    return jnp.clip(array, min=-limit, max=limit).astype(kind)


def setup_inputs(seed: int = 0) -> dict:
    seeds = jax.random.split(jax.random.key(seed), 7)
    return {
        "scalar": draw_scalar(jax.random.fold_in(seeds[6], 71), 0),
        "bin_index": draw_bin_index(jax.random.fold_in(seeds[6], 71), 0),
        "color_table": jnp.clip(jax.random.uniform(seeds[2], (3, NBINS + 1), jnp.float32, 0.099609375, 1.0), 0.099609375, 1.0).astype(jnp.bfloat16),
        "opacity_table": jnp.clip(jnp.exp(jax.random.uniform(seeds[3], (NBINS + 1,), jnp.float32, math.log(0.00049972534), math.log(0.019897461))), 0.00049972534, 0.019897461).astype(jnp.bfloat16),
        "light_dir": bell_draw(seeds[4], (3,), 1.5, 4.0, jnp.float32),
        "view_order": jax.random.permutation(seeds[5], N_GZ).astype(jnp.int32),
    }


def shading_from(field, row_padded, light_dir):
    next_slice = jnp.concatenate([field[1:], field[-1:]], axis=0)
    behind = jnp.concatenate([field[:1], field[:-1]], axis=0)
    grad_depth = next_slice - behind
    grad_rows = row_padded[:, 2:] - row_padded[:, :-2]
    col_padded = jnp.pad(field, ((0, 0), (0, 0), (1, 1)))
    grad_cols = col_padded[:, :, 2:] - col_padded[:, :, :-2]
    facing = grad_depth * light_dir[0] + grad_rows * light_dir[1] + grad_cols * light_dir[2]
    squared = grad_depth * grad_depth + grad_rows * grad_rows + grad_cols * grad_cols
    return 0.25 + 0.75 * facing * facing / (squared + 1.0)


def blend_emission(lower, upper, fraction, shading):
    blended = (1.0 - fraction) * lower + fraction * upper
    opacity = blended[3]
    emitted = (opacity * shading) * blended[:3]
    return emitted, jnp.log1p(-opacity)


def reference(scalar, bin_index, color_table, opacity_table, light_dir, view_order):
    brick_order = jnp.argsort(view_order).astype(jnp.int32)

    def advance(running, position):
        color_sum, keep_sum = running
        brick_id = brick_order[position]
        start = (brick_id * DZ).astype(jnp.int32)
        field = lax.dynamic_slice_in_dim(scalar, start, DZ, 0)
        bin_codes = lax.dynamic_slice_in_dim(bin_index, start, DZ, 0)
        row_padded = jnp.pad(field, ((0, 0), (1, 1), (0, 0)))
        shading = shading_from(field, row_padded, light_dir)
        fraction = field * NBINS - bin_codes.astype(field.dtype)
        lower = jnp.concatenate([color_table[:, bin_codes], opacity_table[bin_codes][None]], axis=0).astype(field.dtype)
        upper_codes = bin_codes + 1
        upper = jnp.concatenate([color_table[:, upper_codes], opacity_table[upper_codes][None]], axis=0).astype(field.dtype)
        emitted, log_keep = blend_emission(lower, upper, fraction, shading)
        passed = jnp.cumsum(log_keep, axis=0) - log_keep
        brick_color = jnp.sum(emitted * jnp.exp(passed)[None], axis=1)
        brick_keep = jnp.sum(log_keep, axis=0)
        return (color_sum + brick_color * jnp.exp(keep_sum)[None], keep_sum + brick_keep), None

    initial = (jnp.zeros((3, NY, W), scalar.dtype), jnp.zeros((NY, W), scalar.dtype))
    finished, unused = lax.scan(advance, initial, jnp.arange(N_GZ, dtype=jnp.int32))
    color_sum, keep_sum = finished
    coverage = 1.0 - jnp.exp(keep_sum)
    image_rgba = jnp.concatenate([color_sum, coverage[None]], axis=0)
    return image_rgba.reshape(4, N_GY, RY, W)
```

```python
import jax
import jax.numpy as jnp
from jax import lax
from jax.experimental import pallas as pl
from jax.experimental.pallas import tpu as pltpu
from jax.sharding import PartitionSpec as P

MESH = pl.DeviceIdType.MESH
GY, GJ, GZ = 8, 8, 8
ROWS = 8
MSG = (ROWS + 2) * 8


def remote(src, dst, send_sem, recv_sem, device):
    return pltpu.make_async_remote_copy(
        src_ref=src, dst_ref=dst, send_sem=send_sem, recv_sem=recv_sem, device_id=device, device_id_type=MESH
    )


def kernel(
    x_ref, tab_ref, light_ref, order_ref, out_ref,
    buf, recv, stage, comp, tabs, ord_v, ord_s,
    ys_sem, yr_sem, zs_sem, zr_sem, xs_sem, xr_sem, o_sem,
):
    me, g = lax.axis_index("gz"), lax.axis_index("gy")
    y, j = me // GJ, me % GJ

    def y_peer(d):
        return (((y + d) % GY) * GJ + j, g)

    def x_peer(d):
        return (y * GJ + (j + d) % GJ, g)

    barrier = pltpu.get_barrier_semaphore()
    for d in range(1, 8):
        pl.semaphore_signal(barrier, inc=1, device_id=y_peer(d), device_id_type=MESH)
        pl.semaphore_signal(barrier, inc=1, device_id=x_peer(d), device_id_type=MESH)

    @pl.when(g > 0)
    def _():
        pl.semaphore_signal(barrier, inc=1, device_id=(me, g - 1), device_id_type=MESH)

    @pl.when(g < GZ - 1)
    def _():
        pl.semaphore_signal(barrier, inc=1, device_id=(me, g + 1), device_id_type=MESH)

    for k in range(2):
        for t in range(8):
            for a in range(8):
                buf[k, pl.ds(8 + 64 * t + a, 8, stride=8), :] = x_ref[k, 8 * t : 8 * t + 8, 128 * a : 128 * a + 128]

    @pl.when(g == 0)
    def _():
        buf[:, 0:8, :] = jnp.zeros((2, 8, 128), jnp.float32)

    @pl.when(g == GZ - 1)
    def _():
        buf[:, 520:528, :] = jnp.zeros((2, 8, 128), jnp.float32)

    for i in range(16):
        tabs[i] = jnp.broadcast_to(tab_ref[i : i + 1, :], (8, 128))

    lane = lax.broadcasted_iota(jnp.int32, (8, 128), 1)
    sub = lax.broadcasted_iota(jnp.int32, (8, 128), 0)
    inverse = jnp.zeros((8, 128), jnp.int32)
    for b in range(64):
        inverse = jnp.where(lane == order_ref[b], b, inverse)
    ord_v[...] = inverse
    order_copy = pltpu.make_async_copy(ord_v, ord_s, o_sem)
    order_copy.start()

    pl.semaphore_wait(barrier, 14 + jnp.where(g > 0, 1, 0) + jnp.where(g < GZ - 1, 1, 0))

    down = remote(buf.at[:, pl.ds(512, 8)], buf.at[:, pl.ds(0, 8)], zs_sem.at[0], zr_sem.at[0], (me, (g + 1) % GZ))
    up = remote(buf.at[:, pl.ds(8, 8)], buf.at[:, pl.ds(520, 8)], zs_sem.at[1], zr_sem.at[1], (me, (g + GZ - 1) % GZ))

    @pl.when(g < GZ - 1)
    def _():
        down.start()

    @pl.when(g > 0)
    def _():
        up.start()

    def y_copy(d):
        t = (y + d) % GY
        return remote(buf.at[:, pl.ds(pl.multiple_of(64 * t, 64), MSG)], recv.at[d], ys_sem.at[d], yr_sem.at[d], y_peer(d))

    order = (1, 7, 2, 6, 3, 5, 4)
    for d in order:
        t = (y + d) % GY

        @pl.when((t > 0) & (t < GY - 1))
        def _():
            y_copy(d).start()

    @pl.when(g > 0)
    def _():
        down.wait_recv()

    @pl.when(g < GZ - 1)
    def _():
        up.wait_recv()

    for d in order:
        t = (y + d) % GY

        @pl.when((t == 0) | (t == GY - 1))
        def _():
            y_copy(d).start()

    l0, l1, l2 = light_ref[0], light_ref[1], light_ref[2]

    def shade(s, up_row, down_row, grad_depth):
        a = pltpu.roll(s, 127, 1)
        right = jnp.where(lane == 127, jnp.where(sub == 7, 0.0, pltpu.roll(a, 7, 0)), a)
        b = pltpu.roll(s, 1, 1)
        left = jnp.where(lane == 0, jnp.where(sub == 0, 0.0, pltpu.roll(b, 1, 0)), b)
        grad_cols = right - left
        grad_rows = down_row - up_row
        facing = grad_depth * l0 + grad_rows * l1 + grad_cols * l2
        squared = grad_depth * grad_depth + grad_rows * grad_rows + grad_cols * grad_cols
        return 0.25 + 0.75 * facing * facing / (squared + 1.0)

    def lookup(s):
        scaled = s * 256.0
        floor = jnp.minimum(jnp.floor(scaled), 255.0)
        fraction = scaled - floor
        code = floor.astype(jnp.int32)
        low = code & 127
        second = code > 127
        out = []
        for c in range(4):
            pair = []
            for w in range(2):
                v0 = jnp.take_along_axis(tabs[4 * c + 2 * w], low, axis=1, mode="promise_in_bounds")
                v1 = jnp.take_along_axis(tabs[4 * c + 2 * w + 1], low, axis=1, mode="promise_in_bounds")
                pair.append(jnp.where(second, v1, v0))
            out.append(pair[0] + fraction * pair[1])
        return out

    def brick(src, base, d):
        def row(i, carry):
            def at(k, r):
                return src[k, pl.ds(pl.multiple_of(base + 8 * (i + r), 8), 8), :]

            s0, s1 = at(0, 1), at(1, 1)
            grad_depth = s1 - s0
            sh0 = shade(s0, at(0, 0), at(0, 2), grad_depth)
            sh1 = shade(s1, at(1, 0), at(1, 2), grad_depth)
            v0, v1 = lookup(s0), lookup(s1)
            keep = 1.0 - v0[3]
            w0 = v0[3] * sh0
            w1 = v1[3] * sh1 * keep
            for c in range(3):
                stage[d, i, c] = w0 * v0[c] + w1 * v1[c]
            stage[d, i, 3] = keep * (1.0 - v1[3])
            return carry

        lax.fori_loop(0, ROWS, row, 0)

    def x_copy(d, e):
        number = ((y + GY - d) % GY) * GJ + j
        return remote(stage.at[d, (j + e) % GJ], comp.at[number], xs_sem.at[d, e], xr_sem.at[d, e], x_peer(e))

    def hand_out(d):
        number = ((y + GY - d) % GY) * GJ + j
        for e in range(1, GJ):
            x_copy(d, e).start()
        comp[number] = stage[d, j]

    brick(buf, 64 * y, 0)
    hand_out(0)

    def step(s, carry):
        d = jnp.where(s % 2 == 1, (s + 1) // 2, GY - s // 2)
        y_copy(d).wait_recv()
        brick(recv.at[d], 0, d)
        hand_out(d)
        return carry

    lax.fori_loop(1, GY, step, 0)

    order_copy.wait()

    def settle(d, carry):
        for e in range(1, GJ):
            x_copy(d, e).wait_recv()
        return carry

    lax.fori_loop(0, GY, settle, 0)

    def composite(p, carry):
        red, green, blue, through = carry
        b = ord_s[0, p]
        red = red + comp[b, 0] * through
        green = green + comp[b, 1] * through
        blue = blue + comp[b, 2] * through
        return red, green, blue, through * comp[b, 3]

    zero = jnp.zeros((8, 128), jnp.float32)
    red, green, blue, through = lax.fori_loop(0, 64, composite, (zero, zero, zero, zero + 1.0), unroll=8)
    out_ref[0] = red
    out_ref[1] = green
    out_ref[2] = blue
    out_ref[3] = 1.0 - through

    def drain(d, carry):
        for e in range(1, GJ):
            x_copy(d, e).wait_send()
        return carry

    lax.fori_loop(0, GY, drain, 0)
    for d in range(1, GY):
        y_copy(d).wait_send()

    @pl.when(g < GZ - 1)
    def _():
        down.wait_send()

    @pl.when(g > 0)
    def _():
        up.wait_send()


def shards(scalar, bin_index, color_table, opacity_table, light_dir, view_order):
    table = jnp.concatenate([color_table, opacity_table[None]], axis=0).astype(jnp.float32)
    lower, upper = table[:, :-1], table[:, 1:]
    tables = jnp.stack([lower, upper - lower], axis=1).reshape(16, 128)
    vmem, smem = pl.BlockSpec(memory_space=pltpu.VMEM), pl.BlockSpec(memory_space=pltpu.SMEM)
    f32, dma = jnp.float32, pltpu.SemaphoreType.DMA
    image = pl.pallas_call(
        kernel,
        out_shape=jax.ShapeDtypeStruct((4, 8, 128), f32),
        in_specs=[vmem, vmem, smem, smem],
        out_specs=vmem,
        scratch_shapes=[
            pltpu.VMEM((2, 528, 128), f32),
            pltpu.VMEM((GY, 2, MSG, 128), f32),
            pltpu.VMEM((GY, ROWS, 4, 8, 128), f32),
            pltpu.VMEM((GY * GJ, 4, 8, 128), f32),
            pltpu.VMEM((16, 8, 128), f32),
            pltpu.VMEM((8, 128), jnp.int32),
            pltpu.SMEM((8, 128), jnp.int32),
            dma((GY,)), dma((GY,)), dma((2,)), dma((2,)), dma((GY, GJ)), dma((GY, GJ)), dma,
        ],
        compiler_params=pltpu.CompilerParams(collective_id=0, has_side_effects=True),
    )(scalar, tables, light_dir, view_order)
    return image.reshape(4, 1, 1, 1024)


def solution(mesh):
    in_specs = (P("gz", "gy", None), P("gz", "gy", None), P(), P(), P(), P())
    out_specs = P(None, "gy", "gz", None)
    return jax.shard_map(shards, mesh=mesh, in_specs=in_specs, out_specs=out_specs, check_vma=False)
```

```python
import jax
import jax.numpy as jnp
from jax import lax
from jax.experimental import pallas as pl
from jax.experimental.pallas import tpu as pltpu
from jax.sharding import PartitionSpec as P

MESH = pl.DeviceIdType.MESH
GY, GJ, GZ = 8, 8, 8
ROWS = 8
NEAR, FAR = (1, 7, 2, 6), (3, 5, 4)
X_ORDER = (4, 3, 5, 2, 6, 1, 7)


def remote(src, dst, send_sem, recv_sem, device):
    return pltpu.make_async_remote_copy(
        src_ref=src, dst_ref=dst, send_sem=send_sem, recv_sem=recv_sem, device_id=device, device_id_type=MESH
    )


def kernel(
    x_ref, color_hbm, opacity_hbm, light_hbm, order_hbm, out_ref,
    color_ref, opacity_ref, light_ref, order_ref,
    xv, zrow, halo, recv, recv_halo, stage, comp, tabs, ord_v, ord_s,
    in_sem, small_sem, ys_sem, yr_sem, hs_sem, hr_sem, zs_sem, zr_sem, xs_sem, xr_sem, o_sem,
):
    me, g = lax.axis_index("gz"), lax.axis_index("gy")
    y, j = me // GJ, me % GJ

    def y_peer(d):
        return (((y + d) % GY) * GJ + j, g)

    def x_peer(d):
        return (y * GJ + (j + d) % GJ, g)

    barrier = pltpu.get_barrier_semaphore()
    for d in (4, 3, 5, 2, 6, 1, 7):
        pl.semaphore_signal(barrier, inc=1, device_id=y_peer(d), device_id_type=MESH)
        pl.semaphore_signal(barrier, inc=1, device_id=x_peer(d), device_id_type=MESH)

    @pl.when(g > 0)
    def _():
        pl.semaphore_signal(barrier, inc=1, device_id=(me, g - 1), device_id_type=MESH)

    @pl.when(g < GZ - 1)
    def _():
        pl.semaphore_signal(barrier, inc=1, device_id=(me, g + 1), device_id_type=MESH)

    load = pltpu.make_async_copy(x_ref, xv, in_sem)
    load.start()
    small = [
        pltpu.make_async_copy(source, target, small_sem.at[i])
        for i, (source, target) in enumerate(
            ((color_hbm, color_ref), (opacity_hbm, opacity_ref), (light_hbm, light_ref), (order_hbm, order_ref))
        )
    ]
    for copy in small:
        copy.start()

    lane = lax.broadcasted_iota(jnp.int32, (8, 128), 1)
    sub = lax.broadcasted_iota(jnp.int32, (8, 128), 0)

    load.wait()
    for k in range(2):
        zrow[0, k] = xv[k, 63:64, :]
        zrow[1, k] = xv[k, 0:1, :]
        for t in range(8):
            if t > 0:
                halo[t, k] = xv[k, 8 * t - 1 : 8 * t, :]
            if t < 7:
                halo[t, 2 + k] = xv[k, 8 * t + 8 : 8 * t + 9, :]

    @pl.when(g == 0)
    def _():
        halo[0, 0:2] = jnp.zeros((2, 1, 1024), jnp.float32)

    @pl.when(g == GZ - 1)
    def _():
        halo[7, 2:4] = jnp.zeros((2, 1, 1024), jnp.float32)

    def fill(c, values):
        for h in range(2):
            lower, upper = values[:, 128 * h : 128 * h + 128], values[:, 128 * h + 1 : 128 * h + 129]
            tabs[4 * c + h] = jnp.broadcast_to(lower, (8, 128))
            tabs[4 * c + 2 + h] = jnp.broadcast_to(upper - lower, (8, 128))

    for copy in small:
        copy.wait()
    colors = color_ref[...].astype(jnp.float32)
    for c in range(3):
        fill(c, colors[c : c + 1])
    fill(3, opacity_ref[...].astype(jnp.float32).reshape(1, 257))

    pl.semaphore_wait(barrier, 14 + jnp.where(g > 0, 1, 0) + jnp.where(g < GZ - 1, 1, 0))

    down = remote(zrow.at[0], halo.at[0, pl.ds(0, 2)], zs_sem.at[0], zr_sem.at[0], (me, (g + 1) % GZ))
    up = remote(zrow.at[1], halo.at[7, pl.ds(2, 2)], zs_sem.at[1], zr_sem.at[1], (me, (g + GZ - 1) % GZ))

    @pl.when(g < GZ - 1)
    def _():
        down.start()

    @pl.when(g > 0)
    def _():
        up.start()

    def y_copy(d):
        t = (y + d) % GY
        rows = x_ref.at[:, pl.ds(pl.multiple_of(ROWS * t, ROWS), ROWS), :]
        return remote(rows, recv.at[d], ys_sem.at[d], yr_sem.at[d], y_peer(d))

    def halo_copy(d):
        return remote(halo.at[(y + d) % GY], recv_halo.at[d], hs_sem.at[d], hr_sem.at[d], y_peer(d))

    def inner_halo(d):
        t = (y + d) % GY

        @pl.when((t > 0) & (t < GY - 1))
        def _():
            halo_copy(d).start()

    for d in NEAR:
        inner_halo(d)
        y_copy(d).start()

    @pl.when(g > 0)
    def _():
        down.wait_recv()

    @pl.when(g < GZ - 1)
    def _():
        up.wait_recv()

    for d in NEAR + FAR:
        t = (y + d) % GY

        @pl.when((t == 0) | (t == GY - 1))
        def _():
            halo_copy(d).start()

    for d in FAR:
        inner_halo(d)
        y_copy(d).start()

    l0, l1, l2 = light_ref[0], light_ref[1], light_ref[2]

    def lookup(s):
        scaled = s * 256.0
        floor = jnp.minimum(jnp.floor(scaled), 255.0)
        fraction = scaled - floor
        code = floor.astype(jnp.int32)
        low = code & 127
        second = code > 127
        out = []
        for c in range(4):
            pair = []
            for w in range(2):
                v0 = jnp.take_along_axis(tabs[4 * c + 2 * w], low, axis=1, mode="promise_in_bounds")
                v1 = jnp.take_along_axis(tabs[4 * c + 2 * w + 1], low, axis=1, mode="promise_in_bounds")
                pair.append(jnp.where(second, v1, v0))
            out.append(pair[0] + fraction * pair[1])
        return out

    first, last, top, bottom = lane == 0, lane == 127, sub == 0, sub == 7

    def brick(main, edge, d):
        cells = [[main(k, a) for a in range(8)] for k in range(2)]
        after = [[pltpu.roll(cells[k][a], 127, 1) for a in range(8)] for k in range(2)]
        before = [[pltpu.roll(cells[k][a], 1, 1) for a in range(8)] for k in range(2)]
        for a in range(8):
            grad_depth = cells[1][a] - cells[0][a]
            shading, looked = [], []
            for k in range(2):
                s = cells[k][a]
                right = jnp.where(last, after[k][a + 1] if a < 7 else 0.0, after[k][a])
                left = jnp.where(first, before[k][a - 1] if a > 0 else 0.0, before[k][a])
                above = jnp.where(top, jnp.broadcast_to(edge(k, a), (8, 128)), pltpu.roll(s, 1, 0))
                below = jnp.where(bottom, jnp.broadcast_to(edge(2 + k, a), (8, 128)), pltpu.roll(s, 7, 0))
                grad_cols, grad_rows = right - left, below - above
                facing = grad_depth * l0 + grad_rows * l1 + grad_cols * l2
                squared = grad_depth * grad_depth + grad_rows * grad_rows + grad_cols * grad_cols
                shading.append(0.25 + 0.75 * facing * facing / (squared + 1.0))
                looked.append(lookup(s))
            v0, v1 = looked
            keep = 1.0 - v0[3]
            w0 = v0[3] * shading[0]
            w1 = v1[3] * shading[1] * keep
            for c in range(3):
                stage[d, pl.ds(8 * c + a, 8, stride=32), :] = w0 * v0[c] + w1 * v1[c]
            stage[d, pl.ds(24 + a, 8, stride=32), :] = keep * (1.0 - v1[3])

    def x_copy(d, e):
        number = ((y + GY - d) % GY) * GJ + j
        rows = stage.at[d, pl.ds(pl.multiple_of(32 * ((j + e) % GJ), 32), 32)]
        return remote(rows, comp.at[number], xs_sem.at[d, e], xr_sem.at[d, e], x_peer(e))

    def hand_out(d):
        number = ((y + GY - d) % GY) * GJ + j
        for e in X_ORDER:
            x_copy(d, e).start()
        comp[number] = stage[d, pl.ds(pl.multiple_of(32 * j, 32), 32)]

    def column(a):
        return slice(128 * a, 128 * a + 128)

    own = pl.ds(pl.multiple_of(ROWS * y, ROWS), ROWS)
    brick(lambda k, a: xv[k, own, column(a)], lambda r, a: halo[y, r, :, column(a)], 0)
    hand_out(0)

    inverse = jnp.zeros((8, 128), jnp.int32)
    for b in range(64):
        inverse = jnp.where(lane == order_ref[b], b, inverse)
    ord_v[...] = inverse
    order_copy = pltpu.make_async_copy(ord_v, ord_s, o_sem)
    order_copy.start()

    def step(s, carry):
        d = jnp.where(s % 2 == 1, (s + 1) // 2, GY - s // 2)
        halo_copy(d).wait_recv()
        y_copy(d).wait_recv()
        brick(lambda k, a: recv[d, k, :, column(a)], lambda r, a: recv_halo[d, r, :, column(a)], d)
        hand_out(d)
        return carry

    lax.fori_loop(1, GY, step, 0)

    order_copy.wait()

    def settle(d, carry):
        for e in X_ORDER:
            x_copy(d, e).wait_recv()
        return carry

    lax.fori_loop(0, GY, settle, 0)

    def composite(p, carry):
        red, green, blue, through = carry
        b = ord_s[0, p]
        red = red + comp[b, 0:8] * through
        green = green + comp[b, 8:16] * through
        blue = blue + comp[b, 16:24] * through
        return red, green, blue, through * comp[b, 24:32]

    zero = jnp.zeros((8, 128), jnp.float32)
    red, green, blue, through = lax.fori_loop(0, 64, composite, (zero, zero, zero, zero + 1.0), unroll=8)
    out_ref[0] = red
    out_ref[1] = green
    out_ref[2] = blue
    out_ref[3] = 1.0 - through

    def drain(d, carry):
        for e in X_ORDER:
            x_copy(d, e).wait_send()
        return carry

    lax.fori_loop(0, GY, drain, 0)
    for d in range(1, GY):
        y_copy(d).wait_send()
        halo_copy(d).wait_send()

    @pl.when(g < GZ - 1)
    def _():
        down.wait_send()

    @pl.when(g > 0)
    def _():
        up.wait_send()


def shards(scalar, bin_index, color_table, opacity_table, light_dir, view_order):
    f32, dma = jnp.float32, pltpu.SemaphoreType.DMA
    image = pl.pallas_call(
        kernel,
        out_shape=jax.ShapeDtypeStruct((4, 8, 128), f32),
        in_specs=[pl.BlockSpec(memory_space=pltpu.HBM)] * 5,
        out_specs=pl.BlockSpec(memory_space=pltpu.VMEM),
        scratch_shapes=[
            pltpu.VMEM(color_table.shape, color_table.dtype),
            pltpu.VMEM(opacity_table.shape, opacity_table.dtype),
            pltpu.SMEM(light_dir.shape, light_dir.dtype),
            pltpu.SMEM(view_order.shape, view_order.dtype),
            pltpu.VMEM((2, 64, 1024), f32),
            pltpu.VMEM((2, 2, 1, 1024), f32),
            pltpu.VMEM((GY, 4, 1, 1024), f32),
            pltpu.VMEM((GY, 2, ROWS, 1024), f32),
            pltpu.VMEM((GY, 4, 1, 1024), f32),
            pltpu.VMEM((GY, ROWS * 32, 128), f32),
            pltpu.VMEM((GY * GJ, 32, 128), f32),
            pltpu.VMEM((16, 8, 128), f32),
            pltpu.VMEM((8, 128), jnp.int32),
            pltpu.SMEM((8, 128), jnp.int32),
            dma, dma((4,)), dma((GY,)), dma((GY,)), dma((GY,)), dma((GY,)), dma((2,)), dma((2,)), dma((GY, GJ)), dma((GY, GJ)), dma,
        ],
        compiler_params=pltpu.CompilerParams(collective_id=0, has_side_effects=True),
    )(scalar, color_table, opacity_table, light_dir, view_order)
    return image.reshape(4, 1, 1, 1024)


def solution(mesh):
    in_specs = (P("gz", "gy", None), P("gz", "gy", None), P(), P(), P(), P())
    out_specs = P(None, "gy", "gz", None)
    return jax.shard_map(shards, mesh=mesh, in_specs=in_specs, out_specs=out_specs, check_vma=False)
```

```python
import jax
import jax.numpy as jnp
from jax import lax
from jax.experimental import pallas as pl
from jax.experimental.pallas import tpu as pltpu
from jax.sharding import PartitionSpec as P

MESH = pl.DeviceIdType.MESH
GY, GJ, GZ = 8, 8, 8
ROWS = 8
NEAR, FAR = (1, 7, 2, 6), (3, 5, 4)
X_ORDER = (4, 3, 5, 2, 6, 1, 7)


def remote(src, dst, send_sem, recv_sem, device):
    return pltpu.make_async_remote_copy(
        src_ref=src, dst_ref=dst, send_sem=send_sem, recv_sem=recv_sem, device_id=device, device_id_type=MESH
    )


def kernel(
    x_ref, color_hbm, opacity_hbm, light_hbm, order_hbm, out_ref,
    color_ref, opacity_ref, light_ref, order_ref,
    xv, zrow, halo, recv, recv_halo, stage, comp, tabs, ord_v, ord_s,
    in_sem, small_sem, ys_sem, yr_sem, hs_sem, hr_sem, zs_sem, zr_sem, xs_sem, xr_sem, o_sem, beyond_sem,
):
    me, g = lax.axis_index("gz"), lax.axis_index("gy")
    y, j = me // GJ, me % GJ

    def y_peer(d):
        return (((y + d) % GY) * GJ + j, g)

    def x_peer(d):
        return (y * GJ + (j + d) % GJ, g)

    barrier = pltpu.get_barrier_semaphore()
    for device in [x_peer(d) for d in X_ORDER] + [y_peer(d) for d in (2, 6, 1, 7)]:
        pl.semaphore_signal(barrier, inc=1, device_id=device, device_id_type=MESH)

    @pl.when(g > 0)
    def _():
        pl.semaphore_signal(barrier, inc=1, device_id=(me, g - 1), device_id_type=MESH)

    @pl.when(g < GZ - 1)
    def _():
        pl.semaphore_signal(barrier, inc=1, device_id=(me, g + 1), device_id_type=MESH)

    load = pltpu.make_async_copy(x_ref, xv, in_sem)
    load.start()
    small = [
        pltpu.make_async_copy(source, target, small_sem.at[i])
        for i, (source, target) in enumerate(
            ((color_hbm, color_ref), (opacity_hbm, opacity_ref), (light_hbm, light_ref), (order_hbm, order_ref))
        )
    ]
    for copy in small:
        copy.start()

    lane = lax.broadcasted_iota(jnp.int32, (8, 128), 1)
    sub = lax.broadcasted_iota(jnp.int32, (8, 128), 0)

    def y_copy(d):
        t = (y + d) % GY
        rows = x_ref.at[:, pl.ds(pl.multiple_of(ROWS * t, ROWS), ROWS), :]
        return remote(rows, recv.at[d], ys_sem, yr_sem.at[d], y_peer(d))

    def halo_copy(d):
        return remote(halo.at[(y + d) % GY], recv_halo.at[d], hs_sem, hr_sem.at[d], y_peer(d))

    def inner_halo(d):
        t = (y + d) % GY

        @pl.when((t > 0) & (t < GY - 1))
        def _():
            halo_copy(d).start()

    pl.semaphore_wait(barrier, 11 + jnp.where(g > 0, 1, 0) + jnp.where(g < GZ - 1, 1, 0))
    pl.semaphore_signal(beyond_sem, inc=1, device_id=y_peer(2), device_id_type=MESH)
    pl.semaphore_signal(beyond_sem, inc=1, device_id=y_peer(6), device_id_type=MESH)
    y_copy(1).start()
    y_copy(7).start()

    load.wait()
    for k in range(2):
        zrow[0, k] = xv[k, 63:64, :]
        zrow[1, k] = xv[k, 0:1, :]

    down = remote(zrow.at[0], halo.at[0, pl.ds(0, 2)], zs_sem.at[0], zr_sem.at[0], (me, (g + 1) % GZ))
    up = remote(zrow.at[1], halo.at[7, pl.ds(2, 2)], zs_sem.at[1], zr_sem.at[1], (me, (g + GZ - 1) % GZ))

    @pl.when(g < GZ - 1)
    def _():
        down.start()

    @pl.when(g > 0)
    def _():
        up.start()

    for k in range(2):
        for t in range(8):
            if t > 0:
                halo[t, k] = xv[k, 8 * t - 1 : 8 * t, :]
            if t < 7:
                halo[t, 2 + k] = xv[k, 8 * t + 8 : 8 * t + 9, :]

    @pl.when(g == 0)
    def _():
        halo[0, 0:2] = jnp.zeros((2, 1, 1024), jnp.float32)

    @pl.when(g == GZ - 1)
    def _():
        halo[7, 2:4] = jnp.zeros((2, 1, 1024), jnp.float32)

    inner_halo(1)
    inner_halo(7)
    for d in (2, 6):
        inner_halo(d)
        y_copy(d).start()

    def fill(c, values):
        for h in range(2):
            lower, upper = values[:, 128 * h : 128 * h + 128], values[:, 128 * h + 1 : 128 * h + 129]
            tabs[4 * c + h] = jnp.broadcast_to(lower, (8, 128))
            tabs[4 * c + 2 + h] = jnp.broadcast_to(upper - lower, (8, 128))

    for copy in small:
        copy.wait()
    colors = color_ref[...].astype(jnp.float32)
    for c in range(3):
        fill(c, colors[c : c + 1])
    fill(3, opacity_ref[...].astype(jnp.float32).reshape(1, 257))

    l0, l1, l2 = light_ref[0], light_ref[1], light_ref[2]

    def lookup(s):
        scaled = s * 256.0
        floor = jnp.minimum(jnp.floor(scaled), 255.0)
        fraction = scaled - floor
        code = floor.astype(jnp.int32)
        low = code & 127
        second = code > 127
        out = []
        for c in range(4):
            pair = []
            for w in range(2):
                v0 = jnp.take_along_axis(tabs[4 * c + 2 * w], low, axis=1, mode="promise_in_bounds")
                v1 = jnp.take_along_axis(tabs[4 * c + 2 * w + 1], low, axis=1, mode="promise_in_bounds")
                pair.append(jnp.where(second, v1, v0))
            out.append(pair[0] + fraction * pair[1])
        return out

    first, last, top, bottom = lane == 0, lane == 127, sub == 0, sub == 7

    def brick(main, edge, d):
        cells = [[main(k, a) for a in range(8)] for k in range(2)]
        after = [[pltpu.roll(cells[k][a], 127, 1) for a in range(8)] for k in range(2)]
        before = [[pltpu.roll(cells[k][a], 1, 1) for a in range(8)] for k in range(2)]
        for a in range(8):
            grad_depth = cells[1][a] - cells[0][a]
            shading, looked = [], []
            for k in range(2):
                s = cells[k][a]
                right = jnp.where(last, after[k][a + 1] if a < 7 else 0.0, after[k][a])
                left = jnp.where(first, before[k][a - 1] if a > 0 else 0.0, before[k][a])
                above = jnp.where(top, jnp.broadcast_to(edge(k, a), (8, 128)), pltpu.roll(s, 1, 0))
                below = jnp.where(bottom, jnp.broadcast_to(edge(2 + k, a), (8, 128)), pltpu.roll(s, 7, 0))
                grad_cols, grad_rows = right - left, below - above
                facing = grad_depth * l0 + grad_rows * l1 + grad_cols * l2
                squared = grad_depth * grad_depth + grad_rows * grad_rows + grad_cols * grad_cols
                shading.append(0.25 + 0.75 * facing * facing / (squared + 1.0))
                looked.append(lookup(s))
            v0, v1 = looked
            keep = 1.0 - v0[3]
            w0 = v0[3] * shading[0]
            w1 = v1[3] * shading[1] * keep
            for c in range(3):
                stage[d, pl.ds(8 * c + a, 8, stride=32), :] = w0 * v0[c] + w1 * v1[c]
            stage[d, pl.ds(24 + a, 8, stride=32), :] = keep * (1.0 - v1[3])

    def x_copy(d, e):
        number = ((y + GY - d) % GY) * GJ + j
        rows = stage.at[d, pl.ds(pl.multiple_of(32 * ((j + e) % GJ), 32), 32)]
        return remote(rows, comp.at[number], xs_sem, xr_sem, x_peer(e))

    def hand_out(d):
        number = ((y + GY - d) % GY) * GJ + j
        for e in X_ORDER:
            x_copy(d, e).start()
        comp[number] = stage[d, pl.ds(pl.multiple_of(32 * j, 32), 32)]

    def column(a):
        return slice(128 * a, 128 * a + 128)

    own = pl.ds(pl.multiple_of(ROWS * y, ROWS), ROWS)

    def band_halos():
        @pl.when(g > 0)
        def _():
            down.wait_recv()

        @pl.when(g < GZ - 1)
        def _():
            up.wait_recv()

    edge = (y == 0) | (y == GY - 1)

    @pl.when(edge)
    def _():
        band_halos()

    brick(lambda k, a: xv[k, own, column(a)], lambda r, a: halo[y, r, :, column(a)], 0)
    pl.semaphore_wait(beyond_sem, 2)

    @pl.when(jnp.logical_not(edge))
    def _():
        band_halos()

    for d in NEAR + FAR:
        t = (y + d) % GY

        @pl.when((t == 0) | (t == GY - 1))
        def _():
            halo_copy(d).start()

    for d in FAR:
        inner_halo(d)
        y_copy(d).start()
    hand_out(0)

    inverse = jnp.zeros((8, 128), jnp.int32)
    for b in range(64):
        inverse = jnp.where(lane == order_ref[b], b, inverse)
    ord_v[...] = inverse
    order_copy = pltpu.make_async_copy(ord_v, ord_s, o_sem)
    order_copy.start()

    def step(s, carry):
        d = jnp.where(s % 2 == 1, (s + 1) // 2, GY - s // 2)
        halo_copy(d).wait_recv()
        y_copy(d).wait_recv()
        brick(lambda k, a: recv[d, k, :, column(a)], lambda r, a: recv_halo[d, r, :, column(a)], d)
        hand_out(d)
        return carry

    lax.fori_loop(1, GY, step, 0)

    order_copy.wait()

    bricks = comp.at[pl.ds(0, 56)]
    pltpu.make_async_copy(bricks, bricks, xr_sem).wait()

    def composite(p, carry):
        red, green, blue, through = carry
        b = ord_s[0, p]
        red = red + comp[b, 0:8] * through
        green = green + comp[b, 8:16] * through
        blue = blue + comp[b, 16:24] * through
        return red, green, blue, through * comp[b, 24:32]

    zero = jnp.zeros((8, 128), jnp.float32)
    red, green, blue, through = lax.fori_loop(0, 64, composite, (zero, zero, zero, zero + 1.0), unroll=8)
    out_ref[0] = red
    out_ref[1] = green
    out_ref[2] = blue
    out_ref[3] = 1.0 - through

    for buffer, semaphore in ((stage, xs_sem), (recv, ys_sem), (recv_halo, hs_sem)):
        sent = buffer.at[pl.ds(0, 7)]
        pltpu.make_async_copy(sent, sent, semaphore).wait()

    @pl.when(g < GZ - 1)
    def _():
        down.wait_send()

    @pl.when(g > 0)
    def _():
        up.wait_send()


def shards(scalar, bin_index, color_table, opacity_table, light_dir, view_order):
    f32, dma = jnp.float32, pltpu.SemaphoreType.DMA
    image = pl.pallas_call(
        kernel,
        out_shape=pltpu.VMEM((4, 8, 128), f32),
        in_specs=[pl.BlockSpec(memory_space=pltpu.HBM)] * 5,
        out_specs=pl.BlockSpec(memory_space=pltpu.VMEM),
        scratch_shapes=[
            pltpu.VMEM(color_table.shape, color_table.dtype),
            pltpu.VMEM(opacity_table.shape, opacity_table.dtype),
            pltpu.SMEM(light_dir.shape, light_dir.dtype),
            pltpu.SMEM(view_order.shape, view_order.dtype),
            pltpu.VMEM((2, 64, 1024), f32),
            pltpu.VMEM((2, 2, 1, 1024), f32),
            pltpu.VMEM((GY, 4, 1, 1024), f32),
            pltpu.VMEM((GY, 2, ROWS, 1024), f32),
            pltpu.VMEM((GY, 4, 1, 1024), f32),
            pltpu.VMEM((GY, ROWS * 32, 128), f32),
            pltpu.VMEM((GY * GJ, 32, 128), f32),
            pltpu.VMEM((16, 8, 128), f32),
            pltpu.VMEM((8, 128), jnp.int32),
            pltpu.SMEM((8, 128), jnp.int32),
            dma, dma((4,)), dma, dma((GY,)), dma, dma((GY,)), dma((2,)), dma((2,)), dma, dma, dma, pltpu.SemaphoreType.REGULAR,
        ],
        compiler_params=pltpu.CompilerParams(collective_id=0, has_side_effects=True),
    )(scalar, color_table, opacity_table, light_dir, view_order)
    return image.reshape(4, 1, 1, 1024)


def solution(mesh):
    in_specs = (P("gz", "gy", None), P("gz", "gy", None), P(), P(), P(), P())
    out_specs = P(None, "gy", "gz", None)
    return jax.shard_map(shards, mesh=mesh, in_specs=in_specs, out_specs=out_specs, check_vma=False)
```

```python
import jax
import jax.numpy as jnp
from jax import lax
from jax.experimental import pallas as pl
from jax.experimental.pallas import tpu as pltpu
from jax.sharding import PartitionSpec as P

MESH = pl.DeviceIdType.MESH
GY, GJ, GZ = 8, 8, 8
ROWS = 8
NEAR, FAR = (1, 7, 2, 6), (3, 5, 4)
X_ORDER = (4, 3, 5, 2, 6, 1, 7)


def remote(src, dst, send_sem, recv_sem, device):
    return pltpu.make_async_remote_copy(
        src_ref=src, dst_ref=dst, send_sem=send_sem, recv_sem=recv_sem, device_id=device, device_id_type=MESH
    )


def kernel(
    x_ref, color_hbm, opacity_hbm, light_hbm, order_hbm, out_ref,
    color_ref, opacity_ref, light_ref, order_ref,
    xv, zrow, halo, recv, recv_halo, stage, comp, tabs, ord_v, ord_s,
    in_sem, small_sem, ys_sem, yr_sem, hs_sem, hr_sem, zs_sem, zr_sem, xs_sem, xr_sem, o_sem, beyond_sem, band_sem,
):
    me, g = lax.axis_index("gz"), lax.axis_index("gy")
    y, j = me // GJ, me % GJ

    def y_peer(d):
        return (((y + d) % GY) * GJ + j, g)

    def x_peer(d):
        return (y * GJ + (j + d) % GJ, g)

    barrier = pltpu.get_barrier_semaphore()
    for device in [x_peer(d) for d in X_ORDER] + [y_peer(d) for d in (2, 6, 1, 7)]:
        pl.semaphore_signal(barrier, inc=1, device_id=device, device_id_type=MESH)

    @pl.when(g < GZ - 1)
    def _():
        pl.semaphore_signal(barrier, inc=1, device_id=(me, g + 1), device_id_type=MESH)

    load = pltpu.make_async_copy(x_ref, xv, in_sem)
    load.start()
    small = [
        pltpu.make_async_copy(source, target, small_sem.at[i])
        for i, (source, target) in enumerate(
            ((color_hbm, color_ref), (opacity_hbm, opacity_ref), (light_hbm, light_ref), (order_hbm, order_ref))
        )
    ]
    for copy in small:
        copy.start()

    lane = lax.broadcasted_iota(jnp.int32, (8, 128), 1)
    sub = lax.broadcasted_iota(jnp.int32, (8, 128), 0)

    def y_copy(d):
        t = (y + d) % GY
        rows = x_ref.at[:, pl.ds(pl.multiple_of(ROWS * t, ROWS), ROWS), :]
        return remote(rows, recv.at[d], ys_sem, yr_sem.at[d], y_peer(d))

    def halo_copy(d):
        return remote(halo.at[(y + d) % GY], recv_halo.at[d], hs_sem, hr_sem.at[d], y_peer(d))

    def inner_halo(d):
        t = (y + d) % GY

        @pl.when((t > 0) & (t < GY - 1))
        def _():
            halo_copy(d).start()

    pl.semaphore_wait(barrier, 11 + jnp.where(g > 0, 1, 0))
    pl.semaphore_signal(beyond_sem, inc=1, device_id=y_peer(2), device_id_type=MESH)
    pl.semaphore_signal(beyond_sem, inc=1, device_id=y_peer(6), device_id_type=MESH)
    y_copy(1).start()
    y_copy(7).start()

    @pl.when(g > 0)
    def _():
        pl.semaphore_signal(band_sem, inc=1, device_id=(me, g - 1), device_id_type=MESH)

    load.wait()
    for k in range(2):
        zrow[0, k] = xv[k, 63:64, :]
        zrow[1, k] = xv[k, 0:1, :]

    down = remote(zrow.at[0], halo.at[0, pl.ds(0, 2)], zs_sem.at[0], zr_sem.at[0], (me, (g + 1) % GZ))
    up = remote(zrow.at[1], halo.at[7, pl.ds(2, 2)], zs_sem.at[1], zr_sem.at[1], (me, (g + GZ - 1) % GZ))

    @pl.when(g > 0)
    def _():
        up.start()

    for k in range(2):
        for t in range(8):
            if t > 0:
                halo[t, k] = xv[k, 8 * t - 1 : 8 * t, :]
            if t < 7:
                halo[t, 2 + k] = xv[k, 8 * t + 8 : 8 * t + 9, :]

    @pl.when(g == 0)
    def _():
        halo[0, 0:2] = jnp.zeros((2, 1, 1024), jnp.float32)

    @pl.when(g == GZ - 1)
    def _():
        halo[7, 2:4] = jnp.zeros((2, 1, 1024), jnp.float32)

    inner_halo(1)
    inner_halo(7)
    for d in (2, 6):
        inner_halo(d)
        y_copy(d).start()

    def fill(c, values):
        for h in range(2):
            lower, upper = values[:, 128 * h : 128 * h + 128], values[:, 128 * h + 1 : 128 * h + 129]
            tabs[4 * c + h] = jnp.broadcast_to(lower, (8, 128))
            tabs[4 * c + 2 + h] = jnp.broadcast_to(upper - lower, (8, 128))

    for copy in small:
        copy.wait()
    colors = color_ref[...].astype(jnp.float32)
    for c in range(3):
        fill(c, colors[c : c + 1])
    fill(3, opacity_ref[...].astype(jnp.float32).reshape(1, 257))

    l0, l1, l2 = light_ref[0], light_ref[1], light_ref[2]

    def lookup(s):
        scaled = s * 256.0
        floor = jnp.minimum(jnp.floor(scaled), 255.0)
        fraction = scaled - floor
        code = floor.astype(jnp.int32)
        low = code & 127
        second = code > 127
        out = []
        for c in range(4):
            pair = []
            for w in range(2):
                v0 = jnp.take_along_axis(tabs[4 * c + 2 * w], low, axis=1, mode="promise_in_bounds")
                v1 = jnp.take_along_axis(tabs[4 * c + 2 * w + 1], low, axis=1, mode="promise_in_bounds")
                pair.append(jnp.where(second, v1, v0))
            out.append(pair[0] + fraction * pair[1])
        return out

    first, last, top, bottom = lane == 0, lane == 127, sub == 0, sub == 7

    def brick(main, edge, d):
        cells = [[main(k, a) for a in range(8)] for k in range(2)]
        after = [[pltpu.roll(cells[k][a], 127, 1) for a in range(8)] for k in range(2)]
        before = [[pltpu.roll(cells[k][a], 1, 1) for a in range(8)] for k in range(2)]
        for a in range(8):
            grad_depth = cells[1][a] - cells[0][a]
            shading, looked = [], []
            for k in range(2):
                s = cells[k][a]
                right = jnp.where(last, after[k][a + 1] if a < 7 else 0.0, after[k][a])
                left = jnp.where(first, before[k][a - 1] if a > 0 else 0.0, before[k][a])
                above = jnp.where(top, jnp.broadcast_to(edge(k, a), (8, 128)), pltpu.roll(s, 1, 0))
                below = jnp.where(bottom, jnp.broadcast_to(edge(2 + k, a), (8, 128)), pltpu.roll(s, 7, 0))
                grad_cols, grad_rows = right - left, below - above
                facing = grad_depth * l0 + grad_rows * l1 + grad_cols * l2
                squared = grad_depth * grad_depth + grad_rows * grad_rows + grad_cols * grad_cols
                shading.append(0.25 + 0.75 * facing * facing / (squared + 1.0))
                looked.append(lookup(s))
            v0, v1 = looked
            keep = 1.0 - v0[3]
            w0 = v0[3] * shading[0]
            w1 = v1[3] * shading[1] * keep
            for c in range(3):
                stage[d, pl.ds(8 * c + a, 8, stride=32), :] = w0 * v0[c] + w1 * v1[c]
            stage[d, pl.ds(24 + a, 8, stride=32), :] = keep * (1.0 - v1[3])

    def x_copy(d, e):
        number = ((y + GY - d) % GY) * GJ + j
        rows = stage.at[d, pl.ds(pl.multiple_of(32 * ((j + e) % GJ), 32), 32)]
        return remote(rows, comp.at[number], xs_sem, xr_sem, x_peer(e))

    def hand_out(d):
        number = ((y + GY - d) % GY) * GJ + j
        for e in X_ORDER:
            x_copy(d, e).start()
        comp[number] = stage[d, pl.ds(pl.multiple_of(32 * j, 32), 32)]

    def column(a):
        return slice(128 * a, 128 * a + 128)

    own = pl.ds(pl.multiple_of(ROWS * y, ROWS), ROWS)

    def band_halos():
        @pl.when(g < GZ - 1)
        def _():
            pl.semaphore_wait(band_sem, 1)
            down.start()

        @pl.when(g > 0)
        def _():
            down.wait_recv()

        @pl.when(g < GZ - 1)
        def _():
            up.wait_recv()

    edge = (y == 0) | (y == GY - 1)

    @pl.when(edge)
    def _():
        band_halos()

    brick(lambda k, a: xv[k, own, column(a)], lambda r, a: halo[y, r, :, column(a)], 0)
    hand_out(0)
    pl.semaphore_wait(beyond_sem, 2)

    @pl.when(jnp.logical_not(edge))
    def _():
        band_halos()

    for d in NEAR + FAR:
        t = (y + d) % GY

        @pl.when((t == 0) | (t == GY - 1))
        def _():
            halo_copy(d).start()

    for d in FAR:
        inner_halo(d)
        y_copy(d).start()

    inverse = jnp.zeros((8, 128), jnp.int32)
    for b in range(64):
        inverse = jnp.where(lane == order_ref[b], b, inverse)
    ord_v[...] = inverse
    order_copy = pltpu.make_async_copy(ord_v, ord_s, o_sem)
    order_copy.start()

    def step(s, carry):
        d = jnp.where(s % 2 == 1, (s + 1) // 2, GY - s // 2)
        halo_copy(d).wait_recv()
        y_copy(d).wait_recv()
        brick(lambda k, a: recv[d, k, :, column(a)], lambda r, a: recv_halo[d, r, :, column(a)], d)
        hand_out(d)
        return carry

    lax.fori_loop(1, GY, step, 0)

    order_copy.wait()

    bricks = comp.at[pl.ds(0, 56)]
    pltpu.make_async_copy(bricks, bricks, xr_sem).wait()

    def composite(p, carry):
        red, green, blue, through = carry
        b = ord_s[0, p]
        red = red + comp[b, 0:8] * through
        green = green + comp[b, 8:16] * through
        blue = blue + comp[b, 16:24] * through
        return red, green, blue, through * comp[b, 24:32]

    zero = jnp.zeros((8, 128), jnp.float32)
    red, green, blue, through = lax.fori_loop(0, 64, composite, (zero, zero, zero, zero + 1.0), unroll=8)
    out_ref[0] = red
    out_ref[1] = green
    out_ref[2] = blue
    out_ref[3] = 1.0 - through

    for buffer, semaphore in ((stage, xs_sem), (recv, ys_sem), (recv_halo, hs_sem)):
        sent = buffer.at[pl.ds(0, 7)]
        pltpu.make_async_copy(sent, sent, semaphore).wait()

    @pl.when(g < GZ - 1)
    def _():
        down.wait_send()

    @pl.when(g > 0)
    def _():
        up.wait_send()


def shards(scalar, bin_index, color_table, opacity_table, light_dir, view_order):
    f32, dma = jnp.float32, pltpu.SemaphoreType.DMA
    image = pl.pallas_call(
        kernel,
        out_shape=pltpu.VMEM((4, 8, 128), f32),
        in_specs=[pl.BlockSpec(memory_space=pltpu.HBM)] * 5,
        out_specs=pl.BlockSpec(memory_space=pltpu.VMEM),
        scratch_shapes=[
            pltpu.VMEM(color_table.shape, color_table.dtype),
            pltpu.VMEM(opacity_table.shape, opacity_table.dtype),
            pltpu.SMEM(light_dir.shape, light_dir.dtype),
            pltpu.SMEM(view_order.shape, view_order.dtype),
            pltpu.VMEM((2, 64, 1024), f32),
            pltpu.VMEM((2, 2, 1, 1024), f32),
            pltpu.VMEM((GY, 4, 1, 1024), f32),
            pltpu.VMEM((GY, 2, ROWS, 1024), f32),
            pltpu.VMEM((GY, 4, 1, 1024), f32),
            pltpu.VMEM((GY, ROWS * 32, 128), f32),
            pltpu.VMEM((GY * GJ, 32, 128), f32),
            pltpu.VMEM((16, 8, 128), f32),
            pltpu.VMEM((8, 128), jnp.int32),
            pltpu.SMEM((8, 128), jnp.int32),
            dma, dma((4,)), dma, dma((GY,)), dma, dma((GY,)), dma((2,)), dma((2,)), dma, dma, dma, pltpu.SemaphoreType.REGULAR,
            pltpu.SemaphoreType.REGULAR,
        ],
        compiler_params=pltpu.CompilerParams(collective_id=0, has_side_effects=True),
    )(scalar, color_table, opacity_table, light_dir, view_order)
    return image.reshape(4, 1, 1, 1024)


def solution(mesh):
    in_specs = (P("gz", "gy", None), P("gz", "gy", None), P(), P(), P(), P())
    out_specs = P(None, "gy", "gz", None)
    return jax.shard_map(shards, mesh=mesh, in_specs=in_specs, out_specs=out_specs, check_vma=False)
```

```python
import jax
import jax.numpy as jnp
from jax import lax
from jax.experimental import pallas as pl
from jax.experimental.pallas import tpu as pltpu
from jax.sharding import PartitionSpec as P

MESH = pl.DeviceIdType.MESH
GY, GJ, GZ = 8, 8, 8
ROWS = 8
NEAR, FAR = (1, 7, 2, 6), (3, 5, 4)
X_ORDER = (4, 3, 5, 2, 6, 1, 7)


def remote(src, dst, send_sem, recv_sem, device):
    return pltpu.make_async_remote_copy(
        src_ref=src, dst_ref=dst, send_sem=send_sem, recv_sem=recv_sem, device_id=device, device_id_type=MESH
    )


def kernel(
    x_ref, color_hbm, opacity_hbm, light_hbm, order_hbm, out_ref,
    color_ref, opacity_ref, light_ref, order_ref,
    xv, zrow, halo, recv, recv_halo, stage, comp, tabs, ord_v, ord_s,
    in_sem, small_sem, ys_sem, yr_sem, hs_sem, hr_sem, zs_sem, zr_sem, xs_sem, xr_sem, o_sem, second_sem, beyond_sem, beside_sem, across_sem, band_sem,
):
    me, g = lax.axis_index("gz"), lax.axis_index("gy")
    y, j = me // GJ, me % GJ

    def y_peer(d):
        return (((y + d) % GY) * GJ + j, g)

    def x_peer(d):
        return (y * GJ + (j + d) % GJ, g)

    barrier = pltpu.get_barrier_semaphore()
    partner = (me + 1 - 2 * (j % 2), g)
    beside = [x_peer(2), x_peer(6), partner]
    for device in [y_peer(1), y_peer(7)] + beside:
        pl.semaphore_signal(barrier, inc=1, device_id=device, device_id_type=MESH)

    @pl.when(g < GZ - 1)
    def _():
        pl.semaphore_signal(barrier, inc=1, device_id=(me, g + 1), device_id_type=MESH)

    load = pltpu.make_async_copy(x_ref, xv, in_sem)
    load.start()
    small = [
        pltpu.make_async_copy(source, target, small_sem.at[i])
        for i, (source, target) in enumerate(
            ((color_hbm, color_ref), (opacity_hbm, opacity_ref), (light_hbm, light_ref), (order_hbm, order_ref))
        )
    ]
    for copy in small:
        copy.start()

    lane = lax.broadcasted_iota(jnp.int32, (8, 128), 1)
    sub = lax.broadcasted_iota(jnp.int32, (8, 128), 0)

    def y_copy(d):
        t = (y + d) % GY
        rows = xv.at[:, pl.ds(pl.multiple_of(ROWS * t, ROWS), ROWS), :]
        return remote(rows, recv.at[d], ys_sem, yr_sem.at[d], y_peer(d))

    def halo_copy(d):
        return remote(halo.at[(y + d) % GY], recv_halo.at[d], hs_sem, hr_sem.at[d], y_peer(d))

    def inner_halo(d):
        t = (y + d) % GY

        @pl.when((t > 0) & (t < GY - 1))
        def _():
            halo_copy(d).start()

    load.wait()
    pl.semaphore_wait(barrier, 5 + jnp.where(g > 0, 1, 0))
    def tell(semaphore, devices):
        for device in devices:
            pl.semaphore_signal(semaphore, inc=1, device_id=device, device_id_type=MESH)

    tell(second_sem, [y_peer(1), y_peer(7)])
    tell(beside_sem, beside)
    y_copy(1).start()
    y_copy(7).start()

    @pl.when(g > 0)
    def _():
        pl.semaphore_signal(band_sem, inc=1, device_id=(me, g - 1), device_id_type=MESH)

    for k in range(2):
        zrow[0, k] = xv[k, 63:64, :]
        zrow[1, k] = xv[k, 0:1, :]

    down = remote(zrow.at[0], halo.at[0, pl.ds(0, 2)], zs_sem.at[0], zr_sem.at[0], (me, (g + 1) % GZ))
    up = remote(zrow.at[1], halo.at[7, pl.ds(2, 2)], zs_sem.at[1], zr_sem.at[1], (me, (g + GZ - 1) % GZ))

    @pl.when(g > 0)
    def _():
        up.start()

    for k in range(2):
        for t in range(8):
            if t > 0:
                halo[t, k] = xv[k, 8 * t - 1 : 8 * t, :]
            if t < 7:
                halo[t, 2 + k] = xv[k, 8 * t + 8 : 8 * t + 9, :]

    @pl.when(g == 0)
    def _():
        halo[0, 0:2] = jnp.zeros((2, 1, 1024), jnp.float32)

    @pl.when(g == GZ - 1)
    def _():
        halo[7, 2:4] = jnp.zeros((2, 1, 1024), jnp.float32)

    inner_halo(1)
    inner_halo(7)
    pl.semaphore_wait(second_sem, 2)
    tell(beyond_sem, [y_peer(2), y_peer(6)])
    for d in (2, 6):
        inner_halo(d)
        y_copy(d).start()
    pl.semaphore_wait(beside_sem, 3)
    tell(across_sem, [partner])

    def fill(c, values):
        for h in range(2):
            lower, upper = values[:, 128 * h : 128 * h + 128], values[:, 128 * h + 1 : 128 * h + 129]
            tabs[4 * c + h] = jnp.broadcast_to(lower, (8, 128))
            tabs[4 * c + 2 + h] = jnp.broadcast_to(upper - lower, (8, 128))

    for copy in small:
        copy.wait()
    colors = color_ref[...].astype(jnp.float32)
    for c in range(3):
        fill(c, colors[c : c + 1])
    fill(3, opacity_ref[...].astype(jnp.float32).reshape(1, 257))

    l0, l1, l2 = light_ref[0], light_ref[1], light_ref[2]

    def lookup(s):
        scaled = s * 256.0
        floor = jnp.minimum(jnp.floor(scaled), 255.0)
        fraction = scaled - floor
        code = floor.astype(jnp.int32)
        low = code & 127
        second = code > 127
        out = []
        for c in range(4):
            pair = []
            for w in range(2):
                v0 = jnp.take_along_axis(tabs[4 * c + 2 * w], low, axis=1, mode="promise_in_bounds")
                v1 = jnp.take_along_axis(tabs[4 * c + 2 * w + 1], low, axis=1, mode="promise_in_bounds")
                pair.append(jnp.where(second, v1, v0))
            out.append(pair[0] + fraction * pair[1])
        return out

    first, last, top, bottom = lane == 0, lane == 127, sub == 0, sub == 7

    def brick(main, edge, d):
        cells = [[main(k, a) for a in range(8)] for k in range(2)]
        after = [[pltpu.roll(cells[k][a], 127, 1) for a in range(8)] for k in range(2)]
        before = [[pltpu.roll(cells[k][a], 1, 1) for a in range(8)] for k in range(2)]
        for a in range(8):
            grad_depth = cells[1][a] - cells[0][a]
            shading, looked = [], []
            for k in range(2):
                s = cells[k][a]
                right = jnp.where(last, after[k][a + 1] if a < 7 else 0.0, after[k][a])
                left = jnp.where(first, before[k][a - 1] if a > 0 else 0.0, before[k][a])
                above = jnp.where(top, jnp.broadcast_to(edge(k, a), (8, 128)), pltpu.roll(s, 1, 0))
                below = jnp.where(bottom, jnp.broadcast_to(edge(2 + k, a), (8, 128)), pltpu.roll(s, 7, 0))
                grad_cols, grad_rows = right - left, below - above
                facing = grad_depth * l0 + grad_rows * l1 + grad_cols * l2
                squared = grad_depth * grad_depth + grad_rows * grad_rows + grad_cols * grad_cols
                shading.append(0.25 + 0.75 * facing * facing / (squared + 1.0))
                looked.append(lookup(s))
            v0, v1 = looked
            keep = 1.0 - v0[3]
            w0 = v0[3] * shading[0]
            w1 = v1[3] * shading[1] * keep
            for c in range(3):
                stage[d, pl.ds(8 * c + a, 8, stride=32), :] = w0 * v0[c] + w1 * v1[c]
            stage[d, pl.ds(24 + a, 8, stride=32), :] = keep * (1.0 - v1[3])

    def x_copy(d, e):
        number = ((y + GY - d) % GY) * GJ + j
        rows = stage.at[d, pl.ds(pl.multiple_of(32 * ((j + e) % GJ), 32), 32)]
        return remote(rows, comp.at[number], xs_sem, xr_sem, x_peer(e))

    def hand_out(d):
        number = ((y + GY - d) % GY) * GJ + j
        for e in X_ORDER:
            x_copy(d, e).start()
        comp[number] = stage[d, pl.ds(pl.multiple_of(32 * j, 32), 32)]

    def column(a):
        return slice(128 * a, 128 * a + 128)

    own = pl.ds(pl.multiple_of(ROWS * y, ROWS), ROWS)

    def band_halos():
        @pl.when(g < GZ - 1)
        def _():
            pl.semaphore_wait(band_sem, 1)
            down.start()

        @pl.when(g > 0)
        def _():
            down.wait_recv()

        @pl.when(g < GZ - 1)
        def _():
            up.wait_recv()

    edge = (y == 0) | (y == GY - 1)

    @pl.when(edge)
    def _():
        band_halos()

    brick(lambda k, a: xv[k, own, column(a)], lambda r, a: halo[y, r, :, column(a)], 0)
    pl.semaphore_wait(across_sem, 1)
    hand_out(0)
    pl.semaphore_wait(beyond_sem, 2)

    @pl.when(jnp.logical_not(edge))
    def _():
        band_halos()

    for d in NEAR + FAR:
        t = (y + d) % GY

        @pl.when((t == 0) | (t == GY - 1))
        def _():
            halo_copy(d).start()

    for d in FAR:
        inner_halo(d)
        y_copy(d).start()

    inverse = jnp.zeros((8, 128), jnp.int32)
    for b in range(64):
        inverse = jnp.where(lane == order_ref[b], b, inverse)
    ord_v[...] = inverse
    order_copy = pltpu.make_async_copy(ord_v, ord_s, o_sem)
    order_copy.start()

    def step(s, carry):
        d = jnp.where(s % 2 == 1, (s + 1) // 2, GY - s // 2)
        halo_copy(d).wait_recv()
        y_copy(d).wait_recv()
        brick(lambda k, a: recv[d, k, :, column(a)], lambda r, a: recv_halo[d, r, :, column(a)], d)
        hand_out(d)
        return carry

    lax.fori_loop(1, GY, step, 0)

    order_copy.wait()

    bricks = comp.at[pl.ds(0, 56)]
    pltpu.make_async_copy(bricks, bricks, xr_sem).wait()

    def composite(p, carry):
        red, green, blue, through = carry
        b = ord_s[0, p]
        red = red + comp[b, 0:8] * through
        green = green + comp[b, 8:16] * through
        blue = blue + comp[b, 16:24] * through
        return red, green, blue, through * comp[b, 24:32]

    zero = jnp.zeros((8, 128), jnp.float32)
    red, green, blue, through = lax.fori_loop(0, 64, composite, (zero, zero, zero, zero + 1.0), unroll=8)
    out_ref[0] = red
    out_ref[1] = green
    out_ref[2] = blue
    out_ref[3] = 1.0 - through

    for buffer, semaphore in ((stage, xs_sem), (recv, ys_sem), (recv_halo, hs_sem)):
        sent = buffer.at[pl.ds(0, 7)]
        pltpu.make_async_copy(sent, sent, semaphore).wait()

    @pl.when(g < GZ - 1)
    def _():
        down.wait_send()

    @pl.when(g > 0)
    def _():
        up.wait_send()


def shards(scalar, bin_index, color_table, opacity_table, light_dir, view_order):
    f32, dma = jnp.float32, pltpu.SemaphoreType.DMA
    image = pl.pallas_call(
        kernel,
        out_shape=pltpu.VMEM((4, 8, 128), f32),
        in_specs=[pl.BlockSpec(memory_space=pltpu.HBM)] * 5,
        out_specs=pl.BlockSpec(memory_space=pltpu.VMEM),
        scratch_shapes=[
            pltpu.VMEM(color_table.shape, color_table.dtype),
            pltpu.VMEM(opacity_table.shape, opacity_table.dtype),
            pltpu.SMEM(light_dir.shape, light_dir.dtype),
            pltpu.SMEM(view_order.shape, view_order.dtype),
            pltpu.VMEM((2, 64, 1024), f32),
            pltpu.VMEM((2, 2, 1, 1024), f32),
            pltpu.VMEM((GY, 4, 1, 1024), f32),
            pltpu.VMEM((GY, 2, ROWS, 1024), f32),
            pltpu.VMEM((GY, 4, 1, 1024), f32),
            pltpu.VMEM((GY, ROWS * 32, 128), f32),
            pltpu.VMEM((GY * GJ, 32, 128), f32),
            pltpu.VMEM((16, 8, 128), f32),
            pltpu.VMEM((8, 128), jnp.int32),
            pltpu.SMEM((8, 128), jnp.int32),
            dma, dma((4,)), dma, dma((GY,)), dma, dma((GY,)), dma((2,)), dma((2,)), dma, dma, dma, pltpu.SemaphoreType.REGULAR,
            pltpu.SemaphoreType.REGULAR, pltpu.SemaphoreType.REGULAR, pltpu.SemaphoreType.REGULAR,
            pltpu.SemaphoreType.REGULAR,
        ],
        compiler_params=pltpu.CompilerParams(collective_id=0, has_side_effects=True),
    )(scalar, color_table, opacity_table, light_dir, view_order)
    return image.reshape(4, 1, 1, 1024)


def solution(mesh):
    in_specs = (P("gz", "gy", None), P("gz", "gy", None), P(), P(), P(), P())
    out_specs = P(None, "gy", "gz", None)
    return jax.shard_map(shards, mesh=mesh, in_specs=in_specs, out_specs=out_specs, check_vma=False)
```

```python
import jax
import jax.numpy as jnp
from jax import lax
from jax.experimental import pallas as pl
from jax.experimental.pallas import tpu as pltpu
from jax.sharding import PartitionSpec as P

MESH = pl.DeviceIdType.MESH
GY, GJ, GZ = 8, 8, 8
ROWS = 8
NEAR, FAR = (1, 7, 2, 6), (3, 5, 4)
X_ORDER = (4, 3, 5, 2, 6, 1, 7)


def remote(src, dst, send_sem, recv_sem, device):
    return pltpu.make_async_remote_copy(
        src_ref=src, dst_ref=dst, send_sem=send_sem, recv_sem=recv_sem, device_id=device, device_id_type=MESH
    )


def kernel(
    x_ref, color_hbm, opacity_hbm, light_hbm, order_hbm, out_ref,
    color_ref, opacity_ref, light_ref, order_ref,
    xv, zrow, halo, recv, recv_halo, stage, comp, tabs, ord_v, ord_s,
    in_sem, small_sem, ys_sem, yr_sem, hs_sem, hr_sem, zs_sem, zr_sem, xs_sem, xr_sem, o_sem, second_sem, beyond_sem, beside_sem, across_sem, band_sem,
):
    me, g = lax.axis_index("gz"), lax.axis_index("gy")
    y, j = me // GJ, me % GJ

    def y_peer(d):
        return (((y + d) % GY) * GJ + j, g)

    def x_peer(d):
        return (y * GJ + (j + d) % GJ, g)

    barrier = pltpu.get_barrier_semaphore()
    partner = (me + 1 - 2 * (j % 2), g)
    beside = [x_peer(2), x_peer(6), partner]
    for device in [y_peer(1), y_peer(7)] + beside:
        pl.semaphore_signal(barrier, inc=1, device_id=device, device_id_type=MESH)

    @pl.when(g < GZ - 1)
    def _():
        pl.semaphore_signal(barrier, inc=1, device_id=(me, g + 1), device_id_type=MESH)

    load = pltpu.make_async_copy(x_ref, xv, in_sem)
    load.start()
    small = [
        pltpu.make_async_copy(source, target, small_sem.at[i])
        for i, (source, target) in enumerate(
            ((color_hbm, color_ref), (opacity_hbm, opacity_ref), (light_hbm, light_ref), (order_hbm, order_ref))
        )
    ]
    for copy in small:
        copy.start()

    lane = lax.broadcasted_iota(jnp.int32, (8, 128), 1)
    sub = lax.broadcasted_iota(jnp.int32, (8, 128), 0)

    def y_copy(d):
        t = (y + d) % GY
        rows = xv.at[:, pl.ds(pl.multiple_of(ROWS * t, ROWS), ROWS), :]
        return remote(rows, recv.at[d], ys_sem, yr_sem.at[d], y_peer(d))

    def halo_copy(d):
        return remote(halo.at[(y + d) % GY], recv_halo.at[d], hs_sem, hr_sem.at[d], y_peer(d))

    def inner_halo(d):
        t = (y + d) % GY

        @pl.when((t > 0) & (t < GY - 1))
        def _():
            halo_copy(d).start()

    load.wait()
    pl.semaphore_wait(barrier, 5 + jnp.where(g > 0, 1, 0))
    def tell(semaphore, devices):
        for device in devices:
            pl.semaphore_signal(semaphore, inc=1, device_id=device, device_id_type=MESH)

    tell(second_sem, [y_peer(1), y_peer(7)])
    tell(beside_sem, beside)
    y_copy(1).start()
    y_copy(7).start()

    @pl.when(g > 0)
    def _():
        pl.semaphore_signal(band_sem, inc=1, device_id=(me, g - 1), device_id_type=MESH)

    for k in range(2):
        zrow[0, k] = xv[k, 63:64, :]
        zrow[1, k] = xv[k, 0:1, :]

    down = remote(zrow.at[0], halo.at[0, pl.ds(0, 2)], zs_sem.at[0], zr_sem.at[0], (me, (g + 1) % GZ))
    up = remote(zrow.at[1], halo.at[7, pl.ds(2, 2)], zs_sem.at[1], zr_sem.at[1], (me, (g + GZ - 1) % GZ))

    @pl.when(g > 0)
    def _():
        up.start()

    for k in range(2):
        for t in range(8):
            if t > 0:
                halo[t, k] = xv[k, 8 * t - 1 : 8 * t, :]
            if t < 7:
                halo[t, 2 + k] = xv[k, 8 * t + 8 : 8 * t + 9, :]

    @pl.when(g == 0)
    def _():
        halo[0, 0:2] = jnp.zeros((2, 1, 1024), jnp.float32)

    @pl.when(g == GZ - 1)
    def _():
        halo[7, 2:4] = jnp.zeros((2, 1, 1024), jnp.float32)

    inner_halo(1)
    inner_halo(7)
    pl.semaphore_wait(second_sem, 2)
    tell(beyond_sem, [y_peer(2), y_peer(6)])
    for d in (2, 6):
        inner_halo(d)
        y_copy(d).start()
    pl.semaphore_wait(beside_sem, 3)
    tell(across_sem, [partner])

    def fill(c, values):
        for h in range(2):
            lower, upper = values[:, 128 * h : 128 * h + 128], values[:, 128 * h + 1 : 128 * h + 129]
            tabs[4 * c + h] = jnp.broadcast_to(lower, (8, 128))
            tabs[4 * c + 2 + h] = jnp.broadcast_to(upper - lower, (8, 128))

    for copy in small:
        copy.wait()
    colors = color_ref[...].astype(jnp.float32)
    for c in range(3):
        fill(c, colors[c : c + 1])
    fill(3, opacity_ref[...].astype(jnp.float32).reshape(1, 257))

    l0, l1, l2 = light_ref[0], light_ref[1], light_ref[2]

    def lookup(s):
        scaled = s * 256.0
        floor = jnp.minimum(jnp.floor(scaled), 255.0)
        fraction = scaled - floor
        code = floor.astype(jnp.int32)
        low = code & 127
        second = code > 127
        out = []
        for c in range(4):
            pair = []
            for w in range(2):
                v0 = jnp.take_along_axis(tabs[4 * c + 2 * w], low, axis=1, mode="promise_in_bounds")
                v1 = jnp.take_along_axis(tabs[4 * c + 2 * w + 1], low, axis=1, mode="promise_in_bounds")
                pair.append(jnp.where(second, v1, v0))
            out.append(pair[0] + fraction * pair[1])
        return out

    first, last, top, bottom = lane == 0, lane == 127, sub == 0, sub == 7

    def brick(main, edge, d):
        cells = [[main(k, a) for a in range(8)] for k in range(2)]
        after = [[pltpu.roll(cells[k][a], 127, 1) for a in range(8)] for k in range(2)]
        before = [[pltpu.roll(cells[k][a], 1, 1) for a in range(8)] for k in range(2)]
        for a in range(8):
            grad_depth = cells[1][a] - cells[0][a]
            shading, looked = [], []
            for k in range(2):
                s = cells[k][a]
                right = jnp.where(last, after[k][a + 1] if a < 7 else 0.0, after[k][a])
                left = jnp.where(first, before[k][a - 1] if a > 0 else 0.0, before[k][a])
                above = jnp.where(top, jnp.broadcast_to(edge(k, a), (8, 128)), pltpu.roll(s, 1, 0))
                below = jnp.where(bottom, jnp.broadcast_to(edge(2 + k, a), (8, 128)), pltpu.roll(s, 7, 0))
                grad_cols, grad_rows = right - left, below - above
                facing = grad_depth * l0 + grad_rows * l1 + grad_cols * l2
                squared = grad_depth * grad_depth + grad_rows * grad_rows + grad_cols * grad_cols
                shading.append(0.25 + 0.75 * facing * facing / (squared + 1.0))
                looked.append(lookup(s))
            v0, v1 = looked
            keep = 1.0 - v0[3]
            w0 = v0[3] * shading[0]
            w1 = v1[3] * shading[1] * keep
            for c in range(3):
                stage[d, pl.ds(8 * c + a, 8, stride=32), :] = w0 * v0[c] + w1 * v1[c]
            stage[d, pl.ds(24 + a, 8, stride=32), :] = keep * (1.0 - v1[3])

    def x_copy(d, e):
        number = ((y + GY - d) % GY) * GJ + j
        rows = stage.at[d, pl.ds(pl.multiple_of(32 * ((j + e) % GJ), 32), 32)]
        return remote(rows, comp.at[number], xs_sem, xr_sem, x_peer(e))

    def hand_out(d):
        number = ((y + GY - d) % GY) * GJ + j
        for e in X_ORDER:
            x_copy(d, e).start()
        comp[number] = stage[d, pl.ds(pl.multiple_of(32 * j, 32), 32)]

    def column(a):
        return slice(128 * a, 128 * a + 128)

    own = pl.ds(pl.multiple_of(ROWS * y, ROWS), ROWS)

    def band_halos():
        @pl.when(g < GZ - 1)
        def _():
            pl.semaphore_wait(band_sem, 1)
            down.start()

        @pl.when(g > 0)
        def _():
            down.wait_recv()

        @pl.when(g < GZ - 1)
        def _():
            up.wait_recv()

    edge = (y == 0) | (y == GY - 1)

    @pl.when(edge)
    def _():
        band_halos()

    brick(lambda k, a: xv[k, own, column(a)], lambda r, a: halo[y, r, :, column(a)], 0)
    pl.semaphore_wait(across_sem, 1)
    hand_out(0)
    pl.semaphore_wait(beyond_sem, 2)

    @pl.when(jnp.logical_not(edge))
    def _():
        band_halos()

    for d in NEAR + FAR:
        t = (y + d) % GY

        @pl.when((t == 0) | (t == GY - 1))
        def _():
            halo_copy(d).start()

    for a, b in zip((3, 5, 4), (3, 4, 5)):
        d = jnp.where(j % 2 == 0, a, b)
        inner_halo(d)
        y_copy(d).start()

    inverse = jnp.zeros((8, 128), jnp.int32)
    for b in range(64):
        inverse = jnp.where(lane == order_ref[b], b, inverse)
    ord_v[...] = inverse
    order_copy = pltpu.make_async_copy(ord_v, ord_s, o_sem)
    order_copy.start()

    def step(s, carry):
        d = jnp.where(s % 2 == 1, (s + 1) // 2, GY - s // 2)
        halo_copy(d).wait_recv()
        y_copy(d).wait_recv()
        brick(lambda k, a: recv[d, k, :, column(a)], lambda r, a: recv_halo[d, r, :, column(a)], d)
        hand_out(d)
        return carry

    lax.fori_loop(1, GY, step, 0)

    order_copy.wait()

    bricks = comp.at[pl.ds(0, 56)]
    pltpu.make_async_copy(bricks, bricks, xr_sem).wait()

    def composite(p, carry):
        red, green, blue, through = carry
        b = ord_s[0, p]
        red = red + comp[b, 0:8] * through
        green = green + comp[b, 8:16] * through
        blue = blue + comp[b, 16:24] * through
        return red, green, blue, through * comp[b, 24:32]

    zero = jnp.zeros((8, 128), jnp.float32)
    red, green, blue, through = lax.fori_loop(0, 64, composite, (zero, zero, zero, zero + 1.0), unroll=8)
    out_ref[0] = red
    out_ref[1] = green
    out_ref[2] = blue
    out_ref[3] = 1.0 - through

    for buffer, semaphore in ((stage, xs_sem), (recv, ys_sem), (recv_halo, hs_sem)):
        sent = buffer.at[pl.ds(0, 7)]
        pltpu.make_async_copy(sent, sent, semaphore).wait()

    @pl.when(g < GZ - 1)
    def _():
        down.wait_send()

    @pl.when(g > 0)
    def _():
        up.wait_send()


def shards(scalar, bin_index, color_table, opacity_table, light_dir, view_order):
    f32, dma = jnp.float32, pltpu.SemaphoreType.DMA
    image = pl.pallas_call(
        kernel,
        out_shape=pltpu.VMEM((4, 8, 128), f32),
        in_specs=[pl.BlockSpec(memory_space=pltpu.HBM)] * 5,
        out_specs=pl.BlockSpec(memory_space=pltpu.VMEM),
        scratch_shapes=[
            pltpu.VMEM(color_table.shape, color_table.dtype),
            pltpu.VMEM(opacity_table.shape, opacity_table.dtype),
            pltpu.SMEM(light_dir.shape, light_dir.dtype),
            pltpu.SMEM(view_order.shape, view_order.dtype),
            pltpu.VMEM((2, 64, 1024), f32),
            pltpu.VMEM((2, 2, 1, 1024), f32),
            pltpu.VMEM((GY, 4, 1, 1024), f32),
            pltpu.VMEM((GY, 2, ROWS, 1024), f32),
            pltpu.VMEM((GY, 4, 1, 1024), f32),
            pltpu.VMEM((GY, ROWS * 32, 128), f32),
            pltpu.VMEM((GY * GJ, 32, 128), f32),
            pltpu.VMEM((16, 8, 128), f32),
            pltpu.VMEM((8, 128), jnp.int32),
            pltpu.SMEM((8, 128), jnp.int32),
            dma, dma((4,)), dma, dma((GY,)), dma, dma((GY,)), dma((2,)), dma((2,)), dma, dma, dma, pltpu.SemaphoreType.REGULAR,
            pltpu.SemaphoreType.REGULAR, pltpu.SemaphoreType.REGULAR, pltpu.SemaphoreType.REGULAR,
            pltpu.SemaphoreType.REGULAR,
        ],
        compiler_params=pltpu.CompilerParams(collective_id=0, has_side_effects=True),
    )(scalar, color_table, opacity_table, light_dir, view_order)
    return image.reshape(4, 1, 1, 1024)


def solution(mesh):
    in_specs = (P("gz", "gy", None), P("gz", "gy", None), P(), P(), P(), P())
    out_specs = P(None, "gy", "gz", None)
    return jax.shard_map(shards, mesh=mesh, in_specs=in_specs, out_specs=out_specs, check_vma=False)
```
